256 devices in a mesh: ha: 16 (over x, y_lo, core), wa: 16 (over z, y_hi).
Axes of the slice: x: 4, y: 4 (y_hi: 2, y_lo: 2; y = y_hi * 2 + y_lo), z: 8, core: 2. Of those that a mesh axis runs over, the one named last changes fastest.
Arguments:
- token_queries: bfloat16 [16, 4, 64, 64, 128], P(None, None, 'ha', 'wa'), may hold values from -48 to 48
- token_keys: bfloat16 [16, 4, 64, 64, 128], P(None, None, 'ha', 'wa'), may hold values from -6 to 6
- token_values: bfloat16 [16, 4, 64, 64, 128], P(None, None, 'ha', 'wa'), may hold values from -6 to 6
Outputs:
- attended: bfloat16 [16, 4, 64, 64, 128], P(None, None, 'ha', 'wa')
The draws below stay inside these ranges and needn't reach their ends.
All inputs are finite; a program needn't handle non-finite values.
Results may differ from the reference program's by a relative error of at most 0.0055.
Values may be sent and summed in bfloat16 or wider, within the bound.
No kernel may reach another device: no remote copies, remote signals or barrier semaphores. Data moves between devices by JAX's collectives and lax.ppermute only.
A program may use at most 64 MiB of HBM per device.

```python
import jax
import jax.numpy as jnp
from jax import lax

DH = 128
H = 16
LF = 4
LH = 64
LW = 64


def pair_draw(key):
    total = LF * LH * LW
    query_key = jax.random.fold_in(key, 11)
    keys_key = jax.random.fold_in(key, 12)
    queries = jnp.clip(3.0 * jax.random.normal(query_key, (H, total, DH), jnp.float32), -18.0, 18.0)
    key_rows = jnp.clip(jax.random.normal(keys_key, (H, total, DH), jnp.float32), -6.0, 6.0)
    return (queries.reshape(H, LF, LH, LW, DH), key_rows.reshape(H, LF, LH, LW, DH))


def draw_token_queries(key, part):
    return pair_draw(key)[0].astype(jnp.bfloat16)


def draw_token_keys(key, part):
    return pair_draw(key)[1].astype(jnp.bfloat16)


def block_scale(key, dims, cuts, low, largest):
    def one(position, parts):
        draws = jax.random.uniform(jax.random.fold_in(jax.random.fold_in(key, 6), position), (parts,), jnp.float32, low / len(cuts), largest / len(cuts))
        return jnp.repeat(jnp.exp(draws), dims[position] // parts).reshape((-1,) + (1,) * (len(dims) - position - 1))

    gain = one(*cuts[0])
    for cut in cuts[1:]:
        gain = gain * one(*cut)
    return gain


def noise(stream_key, shape, spread, bound, shards=(), kind=jnp.bfloat16):
    drawn = jax.random.normal(stream_key, shape, jnp.float32) * spread
    if len(shards) > 0:
        drawn = block_scale(stream_key, shape, shards, -0.22, 0.18) * drawn
    return jnp.clip(drawn, min=-bound, max=bound).astype(kind)


def setup_inputs(seed: int = 0) -> dict:
    key_of = jax.random.split(jax.random.key(seed), 4)
    return {
        "token_queries": draw_token_queries(jax.random.fold_in(key_of[3], 71), 0),
        "token_keys": draw_token_keys(jax.random.fold_in(key_of[3], 71), 0),
        "token_values": noise(key_of[2], (H, LF, LH, LW, DH), 1.0, 6.0, ((2, 16), (3, 16))),
    }


def reference(token_queries, token_keys, token_values):
    heads = token_queries.shape[0]
    head_size = token_queries.shape[-1]
    factor = head_size ** -0.5
    queries = token_queries.reshape(heads, -1, head_size)
    key_rows = token_keys.reshape(heads, -1, head_size)
    value_rows = token_values.reshape(heads, -1, head_size)
    total = queries.shape[1]
    block_size = min(1024, total)

    def one_head(triple):
        head_queries, head_keys, head_values = triple

        def attend_block(query_block):
            scores = jnp.dot(query_block, head_keys.T, preferred_element_type=jnp.float32) * factor
            weights = jnp.exp(scores - jnp.max(scores, axis=1, keepdims=True))
            totals = jnp.sum(weights, axis=1, keepdims=True)
            mixed = jnp.dot(weights.astype(jnp.bfloat16), head_values, preferred_element_type=jnp.float32)
            return (mixed / totals).astype(jnp.bfloat16)

        return lax.map(attend_block, head_queries.reshape(total // block_size, block_size, head_size))

    attended = lax.map(one_head, (queries, key_rows, value_rows))
    return attended.reshape(token_queries.shape)
```

```python
import functools

import jax
import jax.numpy as jnp
from jax import lax
from jax.experimental import pallas as pl
from jax.experimental.pallas import tpu as pltpu
from jax.sharding import Mesh, PartitionSpec as P

AXES = ("x", "yl", "core", "z", "yh")
SIZES = (4, 2, 2, 8, 2)
PLANE = ("x", "yl", "yh")
RING = 8
DH = 128
TOKENS = 64
LOG2E = 1.4426950408889634
FACTOR = DH ** (-0.5) * LOG2E
VMEM = pl.BlockSpec(memory_space=pltpu.VMEM)
PARAMS = pltpu.CompilerParams(vmem_limit_bytes=28 << 20)


def fold_chunk(q, chunk_ref, state):
    keys = chunk_ref[:, :TOKENS, :].reshape(-1, DH)
    values = chunk_ref[:, TOKENS:, :].reshape(-1, DH)
    scores = lax.dot_general(
        keys, q, (((1,), (1,)), ((), ())), preferred_element_type=jnp.float32
    )
    top = jnp.max(scores, axis=0, keepdims=True) * FACTOR
    new_top = top if state is None else jnp.maximum(state[0], top)
    weights = jnp.exp2(scores * FACTOR - new_top)
    total = jnp.sum(weights, axis=0, keepdims=True)
    mixed = lax.dot_general(
        values,
        weights.astype(jnp.bfloat16),
        (((0,), (0,)), ((), ())),
        preferred_element_type=jnp.float32,
    )
    if state is None:
        return (new_top, total, mixed)
    shrink = jnp.exp2(state[0] - new_top)
    return (new_top, state[1] * shrink + total, state[2] * shrink + mixed)


def fold_kernel(n_chunks, first, q_ref, *refs):
    chunks = refs[:n_chunks]
    outs = refs[-3:]
    q = q_ref[...]
    state = None if first else tuple(r[...] for r in refs[n_chunks : n_chunks + 3])
    for chunk in chunks:
        state = fold_chunk(q, chunk, state)
    for ref, value in zip(outs, state):
        ref[...] = value


def fold(q, chunks, state):
    count = q.shape[0]
    first = state is None
    operands = (q, *chunks) + (() if first else tuple(state))
    base = 1 + len(chunks)
    keys = sum(c.shape[0] * TOKENS for c in chunks)
    row = jax.ShapeDtypeStruct((1, count), jnp.float32)
    return pl.pallas_call(
        functools.partial(fold_kernel, len(chunks), first),
        out_shape=(row, row, jax.ShapeDtypeStruct((DH, count), jnp.float32)),
        in_specs=[VMEM] * len(operands),
        out_specs=[VMEM] * 3,
        input_output_aliases={} if first else {base: 0, base + 1: 1, base + 2: 2},
        compiler_params=PARAMS,
        cost_estimate=pl.CostEstimate(
            flops=4 * count * keys * DH,
            bytes_accessed=8 * count * DH + 4 * keys * DH,
            transcendentals=count * keys,
        ),
        name="fold",
    )(*operands)


def last_kernel(n_chunks, q_ref, *refs):
    chunks = refs[:n_chunks]
    top_ref, total_ref, acc_ref = refs[n_chunks : n_chunks + 3]
    away_ref, away_stats_ref, own_ref, own_stats_ref = refs[n_chunks + 3 :]
    half = q_ref.shape[0] // 2
    for away in (True, False):
        cols = slice(half, 2 * half) if away else slice(0, half)
        q = q_ref[cols, :]
        state = (top_ref[:, cols], total_ref[:, cols], acc_ref[:, cols])
        for chunk in chunks:
            state = fold_chunk(q, chunk, state)
        top, total, acc = state
        if away:
            away_ref[...] = (acc / total).astype(jnp.bfloat16)
            away_stats_ref[0:1, :] = top
            away_stats_ref[1:2, :] = total
        else:
            own_ref[...] = acc
            own_stats_ref[0:1, :] = top
            own_stats_ref[1:2, :] = total


def last(q, chunks, state):
    half = q.shape[0] // 2
    operands = (q, *chunks, *state)
    stats = jax.ShapeDtypeStruct((2, half), jnp.float32)
    keys = sum(c.shape[0] * TOKENS for c in chunks)
    return pl.pallas_call(
        functools.partial(last_kernel, len(chunks)),
        out_shape=(
            jax.ShapeDtypeStruct((DH, half), jnp.bfloat16),
            stats,
            jax.ShapeDtypeStruct((DH, half), jnp.float32),
            stats,
        ),
        in_specs=[VMEM] * len(operands),
        out_specs=[VMEM] * 4,
        compiler_params=PARAMS,
        cost_estimate=pl.CostEstimate(
            flops=8 * half * keys * DH,
            bytes_accessed=16 * half * DH + 4 * keys * DH,
            transcendentals=2 * half * keys,
        ),
        name="last",
    )(*operands)


def join_kernel(own_ref, own_stats_ref, other_ref, other_stats_ref, out_ref):
    own_top, own_total = own_stats_ref[0:1, :], own_stats_ref[1:2, :]
    other_top, other_total = other_stats_ref[0:1, :], other_stats_ref[1:2, :]
    top = jnp.maximum(own_top, other_top)
    own_scale = jnp.exp2(own_top - top)
    other_scale = other_total * jnp.exp2(other_top - top)
    total = own_total * own_scale + other_scale
    joined = (
        own_ref[...] * own_scale + other_ref[...].astype(jnp.float32) * other_scale
    ) / total
    out_ref[...] = joined.T.astype(jnp.bfloat16)


def join(own, own_stats, other, other_stats):
    return pl.pallas_call(
        join_kernel,
        out_shape=jax.ShapeDtypeStruct(own.shape[::-1], jnp.bfloat16),
        in_specs=[VMEM] * 4,
        out_specs=VMEM,
        compiler_params=PARAMS,
        name="join",
    )(own, own_stats, other, other_stats)


def shift(block, axis, distance, size):
    return lax.ppermute(block, axis, [(i, (i + distance) % size) for i in range(size)])


def shards(token_queries, token_keys, token_values):
    shape = token_queries.shape
    heads = shape[0]
    flat = [a.reshape(heads, TOKENS, DH) for a in (token_queries, token_keys, token_values)]
    sent = jnp.concatenate(flat, axis=1)
    got = lax.all_to_all(sent, PLANE, split_axis=0, concat_axis=0, tiled=True)
    own_q = got[:, :TOKENS].reshape(heads * TOKENS, DH)
    chunk_a = got[: heads // 2, TOKENS:]
    chunk_b = got[heads // 2 :, TOKENS:]
    other_q = shift(own_q, "core", 1, 2)
    q = jnp.concatenate([own_q, other_q], axis=0)

    state = fold(q, (chunk_a, chunk_b), None)
    right_a = left_a = chunk_a
    right_b = left_b = chunk_b
    for step in range(1, RING // 2):
        right_a, left_a = shift(right_a, "z", 1, RING), shift(left_a, "z", -1, RING)
        right_b, left_b = shift(right_b, "z", 1, RING), shift(left_b, "z", -1, RING)
        state = fold(q, (right_a, left_a), state)
        state = fold(q, (right_b, left_b), state)
    right_a = shift(right_a, "z", 1, RING)
    left_b = shift(left_b, "z", -1, RING)
    away, away_stats, own, own_stats = last(q, (right_a, left_b), state)
    other, other_stats = shift((away, away_stats), "core", 1, 2)
    rows = join(own, own_stats, other, other_stats)
    back = lax.all_to_all(
        rows.reshape(heads, TOKENS, DH), PLANE, split_axis=0, concat_axis=0, tiled=True
    )
    return back.reshape(shape)


def solution(mesh):
    fine = Mesh(mesh.devices.reshape(SIZES), AXES)
    placed = P(None, None, ("x", "yl", "core"), ("z", "yh"), None)
    return jax.shard_map(
        shards,
        mesh=fine,
        in_specs=(placed, placed, placed),
        out_specs=placed,
        check_vma=False,
    )
```

```python
import functools

import jax
import jax.numpy as jnp
from jax import lax
from jax.experimental import pallas as pl
from jax.experimental.pallas import tpu as pltpu
from jax.sharding import Mesh, PartitionSpec as P

AXES = ("x", "yl", "core", "z", "yh")
SIZES = (4, 2, 2, 8, 2)
PLANE = ("x", "yl", "yh")
RING = 8
DH = 128
TOKENS = 64
LOG2E = 1.4426950408889634
FACTOR = DH ** (-0.5) * LOG2E
LIMIT = 2.0**100
TILE = 256
COST_SCALE = 10
VMEM = pl.BlockSpec(memory_space=pltpu.VMEM)
PARAMS = pltpu.CompilerParams(vmem_limit_bytes=28 << 20)


def dot(left, right, left_dim, right_dim):
    return lax.dot_general(
        left,
        right,
        (((left_dim,), (right_dim,)), ((), ())),
        preferred_element_type=jnp.float32,
    )


def fold_chunk(q, chunk_ref, state, exact):
    keys = chunk_ref[:, :TOKENS, :].reshape(-1, DH)
    values = chunk_ref[:, TOKENS:, :].reshape(-1, DH)
    scores = dot(keys, q, 1, 1)
    shift_row = None if state is None else state[0]
    shrink = None
    if exact:
        top = jnp.max(scores, axis=0, keepdims=True) * FACTOR
        if state is not None:
            top = jnp.maximum(shift_row, top)
            shrink = jnp.exp2(shift_row - top)
        shift_row = top
    weights = jnp.exp2(scores * FACTOR - shift_row)
    total = jnp.sum(weights, axis=0, keepdims=True)
    mixed = dot(values, weights.astype(jnp.bfloat16), 0, 0)
    if state is None:
        return (shift_row, total, mixed)
    if shrink is None:
        return (shift_row, state[1] + total, state[2] + mixed)
    return (shift_row, state[1] * shrink + total, state[2] * shrink + mixed)


def cost(queries, chunks):
    keys = sum(c.shape[0] * TOKENS for c in chunks)
    return pl.CostEstimate(
        flops=COST_SCALE * queries * keys * DH,
        bytes_accessed=4 * keys * DH,
        transcendentals=0,
    )


def fold_kernel(n_chunks, first, q_ref, *refs):
    chunks = refs[:n_chunks]
    state = None if first else tuple(r[...] for r in refs[n_chunks : n_chunks + 3])
    for chunk in chunks:
        state = fold_chunk(q_ref[...], chunk, state, state is None)
    for ref, value in zip(refs[-3:], state):
        ref[...] = value


def fold(q, chunks, state):
    count = q.shape[0]
    first = state is None
    operands = (q, *chunks) + (() if first else tuple(state))
    base = 1 + len(chunks)
    row = jax.ShapeDtypeStruct((1, count), jnp.float32)
    return pl.pallas_call(
        functools.partial(fold_kernel, len(chunks), first),
        out_shape=(row, row, jax.ShapeDtypeStruct((DH, count), jnp.float32)),
        in_specs=[VMEM] * len(operands),
        out_specs=[VMEM] * 3,
        input_output_aliases={} if first else {base: 0, base + 1: 1, base + 2: 2},
        compiler_params=PARAMS,
        cost_estimate=cost(count, chunks),
        name="fold",
    )(*operands)


def last_kernel(n_new, n_all, away, q_ref, *refs):
    chunks = refs[:n_all]
    row_refs = refs[n_all : n_all + 3]
    acc_out, stats_out = refs[n_all + 3 :]
    half = q_ref.shape[0] // 2
    start = half if away else 0

    def finish(state, cols):
        top, total, acc = state
        acc_out[:, cols] = (acc / total).astype(jnp.bfloat16) if away else acc
        stats_out[0:1, cols] = top
        stats_out[1:2, cols] = total

    cols = slice(start, start + half)
    state = tuple(r[:, cols] for r in row_refs)
    for chunk in chunks[:n_new]:
        state = fold_chunk(q_ref[cols, :], chunk, state, False)
    finish(state, slice(0, half))

    @pl.when(jnp.logical_not(jnp.max(state[1]) < LIMIT))
    def _():
        def tile(i, carry):
            at = pl.multiple_of(i * TILE, TILE)
            q = q_ref[pl.ds(start + at, TILE), :]
            again = None
            for chunk in chunks:
                again = fold_chunk(q, chunk, again, True)
            finish(again, pl.ds(at, TILE))
            return carry

        lax.fori_loop(0, half // TILE, tile, 0)


def last(q, new, old, state, away):
    half = q.shape[0] // 2
    operands = (q, *new, *old, *state)
    return pl.pallas_call(
        functools.partial(last_kernel, len(new), len(new) + len(old), away),
        out_shape=(
            jax.ShapeDtypeStruct((DH, half), jnp.bfloat16 if away else jnp.float32),
            jax.ShapeDtypeStruct((2, half), jnp.float32),
        ),
        in_specs=[VMEM] * len(operands),
        out_specs=[VMEM] * 2,
        compiler_params=PARAMS,
        cost_estimate=cost(half, new),
        name="last_away" if away else "last_own",
    )(*operands)


def join_kernel(own_ref, own_stats_ref, other_ref, other_stats_ref, out_ref):
    own_top, own_total = own_stats_ref[0:1, :], own_stats_ref[1:2, :]
    other_top, other_total = other_stats_ref[0:1, :], other_stats_ref[1:2, :]
    top = jnp.maximum(own_top, other_top)
    own_scale = jnp.exp2(own_top - top)
    other_scale = other_total * jnp.exp2(other_top - top)
    total = own_total * own_scale + other_scale
    joined = (
        own_ref[...] * own_scale + other_ref[...].astype(jnp.float32) * other_scale
    ) / total
    out_ref[...] = joined.T.astype(jnp.bfloat16)


def join(own, own_stats, other, other_stats):
    return pl.pallas_call(
        join_kernel,
        out_shape=jax.ShapeDtypeStruct(own.shape[::-1], jnp.bfloat16),
        in_specs=[VMEM] * 4,
        out_specs=VMEM,
        compiler_params=PARAMS,
        name="join",
    )(own, own_stats, other, other_stats)


def shift(block, axis, distance, size):
    return lax.ppermute(block, axis, [(i, (i + distance) % size) for i in range(size)])


def shards(token_queries, token_keys, token_values):
    shape = token_queries.shape
    heads = shape[0]
    flat = [a.reshape(heads, TOKENS, DH) for a in (token_queries, token_keys, token_values)]
    sent = jnp.concatenate(flat, axis=1)
    got = lax.all_to_all(sent, PLANE, split_axis=0, concat_axis=0, tiled=True)
    own_q = got[:, :TOKENS].reshape(heads * TOKENS, DH)
    chunk_a = got[: heads // 2, TOKENS:]
    chunk_b = got[heads // 2 :, TOKENS:]
    other_q = shift(own_q, "core", 1, 2)
    q = jnp.concatenate([own_q, other_q], axis=0)

    state = fold(q, (chunk_a, chunk_b), None)
    right_a = left_a = chunk_a
    right_b = left_b = chunk_b
    seen = [chunk_a, chunk_b]
    for step in range(1, RING // 2):
        right_a, left_b = shift(right_a, "z", 1, RING), shift(left_b, "z", -1, RING)
        right_b, left_a = shift(right_b, "z", 1, RING), shift(left_a, "z", -1, RING)
        right_a, left_b, state = lax.optimization_barrier((right_a, left_b, state))
        state = fold(q, (right_a, left_b), state)
        right_b, left_a, state = lax.optimization_barrier((right_b, left_a, state))
        state = fold(q, (right_b, left_a), state)
        seen += [right_a, left_b, right_b, left_a]
    right_a, left_b = shift(right_a, "z", 1, RING), shift(left_b, "z", -1, RING)
    away, away_stats = last(q, (right_a, left_b), seen, state, True)
    other, other_stats = shift((away, away_stats), "core", 1, 2)
    own, own_stats = last(q, (right_a, left_b), seen, state, False)
    rows = join(own, own_stats, other, other_stats)
    back = lax.all_to_all(
        rows.reshape(heads, TOKENS, DH), PLANE, split_axis=0, concat_axis=0, tiled=True
    )
    return back.reshape(shape)


def solution(mesh):
    fine = Mesh(mesh.devices.reshape(SIZES), AXES)
    placed = P(None, None, ("x", "yl", "core"), ("z", "yh"), None)
    return jax.shard_map(
        shards,
        mesh=fine,
        in_specs=(placed, placed, placed),
        out_specs=placed,
        check_vma=False,
    )
```

```python
import functools

import jax
import jax.numpy as jnp
from jax import lax
from jax.experimental import pallas as pl
from jax.experimental.pallas import tpu as pltpu
from jax.sharding import Mesh, PartitionSpec as P

AXES = ("x", "yl", "core", "z", "yh")
SIZES = (4, 2, 2, 8, 2)
PLANE = ("x", "yl", "yh")
RING = 8
DH = 128
TOKENS = 64
LOG2E = 1.4426950408889634
FACTOR = DH ** (-0.5) * LOG2E
LIMIT = 2.0**100
TILE = 256
COST_SCALE = 10
VMEM = pl.BlockSpec(memory_space=pltpu.VMEM)
PARAMS = pltpu.CompilerParams(vmem_limit_bytes=28 << 20)


def dot(left, right, left_dim, right_dim):
    return lax.dot_general(
        left,
        right,
        (((left_dim,), (right_dim,)), ((), ())),
        preferred_element_type=jnp.float32,
    )


def fold_chunk(q, chunk_ref, state, exact):
    keys = chunk_ref[:, :TOKENS, :].reshape(-1, DH)
    values = chunk_ref[:, TOKENS:, :].reshape(-1, DH)
    scores = dot(keys, q, 1, 1)
    shift_row = None if state is None else state[0]
    shrink = None
    if exact:
        top = jnp.max(scores, axis=0, keepdims=True) * FACTOR
        if state is not None:
            top = jnp.maximum(shift_row, top)
            shrink = jnp.exp2(shift_row - top)
        shift_row = top
    weights = jnp.exp2(scores * FACTOR - shift_row)
    total = jnp.sum(weights, axis=0, keepdims=True)
    mixed = dot(values, weights.astype(jnp.bfloat16), 0, 0)
    if state is None:
        return (shift_row, total, mixed)
    if shrink is None:
        return (shift_row, state[1] + total, state[2] + mixed)
    return (shift_row, state[1] * shrink + total, state[2] * shrink + mixed)


def cost(queries, chunks):
    keys = sum(c.shape[0] * TOKENS for c in chunks)
    return pl.CostEstimate(
        flops=COST_SCALE * queries * keys * DH,
        bytes_accessed=4 * keys * DH,
        transcendentals=0,
    )


def fold_kernel(n_chunks, first, q_ref, *refs):
    chunks = refs[:n_chunks]
    state = None if first else tuple(r[...] for r in refs[n_chunks : n_chunks + 3])
    for chunk in chunks:
        state = fold_chunk(q_ref[...], chunk, state, state is None)
    for ref, value in zip(refs[-3:], state):
        ref[...] = value


def fold(q, chunks, state):
    count = q.shape[0]
    first = state is None
    operands = (q, *chunks) + (() if first else tuple(state))
    base = 1 + len(chunks)
    row = jax.ShapeDtypeStruct((1, count), jnp.float32)
    return pl.pallas_call(
        functools.partial(fold_kernel, len(chunks), first),
        out_shape=(row, row, jax.ShapeDtypeStruct((DH, count), jnp.float32)),
        in_specs=[VMEM] * len(operands),
        out_specs=[VMEM] * 3,
        input_output_aliases={} if first else {base: 0, base + 1: 1, base + 2: 2},
        compiler_params=PARAMS,
        cost_estimate=cost(count, chunks),
        name="fold",
    )(*operands)


def last_kernel(n_new, n_all, away, q_ref, *refs):
    chunks = refs[:n_all]
    row_refs = refs[n_all : n_all + 3]
    acc_out, stats_out = refs[n_all + 3 :]
    half = q_ref.shape[0] // 2
    start = half if away else 0

    def finish(state, cols):
        top, total, acc = state
        acc_out[:, cols] = (acc / total).astype(jnp.bfloat16) if away else acc
        stats_out[0:1, cols] = top
        stats_out[1:2, cols] = total

    cols = slice(start, start + half)
    state = tuple(r[:, cols] for r in row_refs)
    for chunk in chunks[:n_new]:
        state = fold_chunk(q_ref[cols, :], chunk, state, False)
    finish(state, slice(0, half))

    @pl.when(jnp.logical_not(jnp.max(state[1]) < LIMIT))
    def _():
        def tile(i, carry):
            at = pl.multiple_of(i * TILE, TILE)
            q = q_ref[pl.ds(start + at, TILE), :]
            again = None
            for chunk in chunks:
                again = fold_chunk(q, chunk, again, True)
            finish(again, pl.ds(at, TILE))
            return carry

        lax.fori_loop(0, half // TILE, tile, 0)


def last(q, new, old, state, away):
    half = q.shape[0] // 2
    operands = (q, *new, *old, *state)
    return pl.pallas_call(
        functools.partial(last_kernel, len(new), len(new) + len(old), away),
        out_shape=(
            jax.ShapeDtypeStruct((DH, half), jnp.bfloat16 if away else jnp.float32),
            jax.ShapeDtypeStruct((2, half), jnp.float32),
        ),
        in_specs=[VMEM] * len(operands),
        out_specs=[VMEM] * 2,
        compiler_params=PARAMS,
        cost_estimate=cost(half, new),
        name="last_away" if away else "last_own",
    )(*operands)


def join_kernel(own_ref, own_stats_ref, other_ref, other_stats_ref, out_ref):
    own_top, own_total = own_stats_ref[0:1, :], own_stats_ref[1:2, :]
    other_top, other_total = other_stats_ref[0:1, :], other_stats_ref[1:2, :]
    top = jnp.maximum(own_top, other_top)
    own_scale = jnp.exp2(own_top - top)
    other_scale = other_total * jnp.exp2(other_top - top)
    total = own_total * own_scale + other_scale
    joined = (
        own_ref[...] * own_scale + other_ref[...].astype(jnp.float32) * other_scale
    ) / total
    out_ref[...] = joined.T.astype(jnp.bfloat16)


def join(own, own_stats, other, other_stats):
    return pl.pallas_call(
        join_kernel,
        out_shape=jax.ShapeDtypeStruct(own.shape[::-1], jnp.bfloat16),
        in_specs=[VMEM] * 4,
        out_specs=VMEM,
        compiler_params=PARAMS,
        name="join",
    )(own, own_stats, other, other_stats)


def shift(block, axis, distance, size):
    return lax.ppermute(block, axis, [(i, (i + distance) % size) for i in range(size)])


def shards(token_queries, token_keys, token_values):
    shape = token_queries.shape
    heads = shape[0]
    flat = [a.reshape(heads, TOKENS, DH) for a in (token_queries, token_keys, token_values)]
    sent = jnp.concatenate(flat, axis=1)
    got = lax.all_to_all(sent, PLANE, split_axis=0, concat_axis=0, tiled=True)
    own_q = got[:, :TOKENS].reshape(heads * TOKENS, DH)
    chunk_a = got[: heads // 2, TOKENS:]
    chunk_b = got[heads // 2 :, TOKENS:]
    other_q = shift(own_q, "core", 1, 2)
    q = jnp.concatenate([own_q, other_q], axis=0)

    right_a, left_b = shift(chunk_a, "z", 1, RING), shift(chunk_b, "z", -1, RING)
    q, chunk_a, chunk_b = lax.optimization_barrier((q, chunk_a, chunk_b))
    right_b, left_a = shift(chunk_b, "z", 1, RING), shift(chunk_a, "z", -1, RING)
    state = fold(q, (chunk_a, chunk_b), None)
    seen = [chunk_a, chunk_b]
    for step in range(1, RING // 2):
        if step > 1:
            right_a, left_b = shift(right_a, "z", 1, RING), shift(left_b, "z", -1, RING)
            right_b, left_a = shift(right_b, "z", 1, RING), shift(left_a, "z", -1, RING)
        right_a, left_b, state = lax.optimization_barrier((right_a, left_b, state))
        state = fold(q, (right_a, left_b), state)
        right_b, left_a, state = lax.optimization_barrier((right_b, left_a, state))
        state = fold(q, (right_b, left_a), state)
        seen += [right_a, left_b, right_b, left_a]
    right_a, left_b = shift(right_a, "z", 1, RING), shift(left_b, "z", -1, RING)
    away, away_stats = last(q, (right_a, left_b), seen, state, True)
    other, other_stats = shift((away, away_stats), "core", 1, 2)
    own, own_stats = last(q, (right_a, left_b), seen, state, False)
    rows = join(own, own_stats, other, other_stats)
    back = lax.all_to_all(
        rows.reshape(shape), PLANE, split_axis=0, concat_axis=0, tiled=True
    )
    return back


def solution(mesh):
    fine = Mesh(mesh.devices.reshape(SIZES), AXES)
    placed = P(None, None, ("x", "yl", "core"), ("z", "yh"), None)
    return jax.shard_map(
        shards,
        mesh=fine,
        in_specs=(placed, placed, placed),
        out_specs=placed,
        check_vma=False,
    )
```

```python
import functools

import jax
import jax.numpy as jnp
from jax import lax
from jax.experimental import pallas as pl
from jax.experimental.pallas import tpu as pltpu
from jax.sharding import Mesh, PartitionSpec as P

AXES = ("x", "yl", "core", "z", "yh")
SIZES = (4, 2, 2, 8, 2)
PLANE = ("x", "yl", "yh")
RING = 8
DH = 128
TOKENS = 64
LOG2E = 1.4426950408889634
FACTOR = DH ** (-0.5) * LOG2E
LIMIT = 2.0**100
TILE = 128
WIDTH = 1024
COST_SCALE = 10
VMEM = pl.BlockSpec(memory_space=pltpu.VMEM)
PARAMS = pltpu.CompilerParams(vmem_limit_bytes=28 << 20)


def dot(left, right, left_dim, right_dim):
    return lax.dot_general(
        left,
        right,
        (((left_dim,), (right_dim,)), ((), ())),
        preferred_element_type=jnp.float32,
    )


def fold_chunk(q, chunk_ref, state, exact):
    keys = chunk_ref[:, :TOKENS, :].reshape(-1, DH)
    values = chunk_ref[:, TOKENS:, :].reshape(-1, DH)
    scores = dot(keys, q, 1, 1)
    shift_row = None if state is None else state[0]
    shrink = None
    if exact:
        top = jnp.max(scores, axis=0, keepdims=True) * FACTOR
        if state is not None:
            top = jnp.maximum(shift_row, top)
            shrink = jnp.exp2(shift_row - top)
        shift_row = top
    weights = jnp.exp2(scores * FACTOR - shift_row)
    total = jnp.sum(weights, axis=0, keepdims=True)
    mixed = dot(values, weights.astype(jnp.bfloat16), 0, 0)
    if state is None:
        return (shift_row, total, mixed)
    if shrink is None:
        return (shift_row, state[1] + total, state[2] + mixed)
    return (shift_row, state[1] * shrink + total, state[2] * shrink + mixed)


def cost(queries, chunks):
    keys = sum(c.shape[0] * TOKENS for c in chunks)
    return pl.CostEstimate(
        flops=COST_SCALE * queries * keys * DH,
        bytes_accessed=4 * keys * DH,
        transcendentals=0,
    )


def each_tile(count, width, body):
    def step(i, carry):
        body(pl.multiple_of(i * width, width))
        return carry

    lax.fori_loop(0, count // width, step, 0)


def fold_kernel(n_chunks, first, q_ref, *refs):
    chunks = refs[:n_chunks]

    def tile(at):
        cols = pl.ds(at, WIDTH)
        state = None if first else tuple(r[:, cols] for r in refs[n_chunks : n_chunks + 3])
        for chunk in chunks:
            state = fold_chunk(q_ref[cols, :], chunk, state, state is None)
        for ref, value in zip(refs[-3:], state):
            ref[:, cols] = value

    each_tile(q_ref.shape[0], WIDTH, tile)


def fold(q, chunks, state):
    count = q.shape[0]
    first = state is None
    operands = (q, *chunks) + (() if first else tuple(state))
    base = 1 + len(chunks)
    row = jax.ShapeDtypeStruct((1, count), jnp.float32)
    return pl.pallas_call(
        functools.partial(fold_kernel, len(chunks), first),
        out_shape=(row, row, jax.ShapeDtypeStruct((DH, count), jnp.float32)),
        in_specs=[VMEM] * len(operands),
        out_specs=[VMEM] * 3,
        input_output_aliases={} if first else {base: 0, base + 1: 1, base + 2: 2},
        compiler_params=PARAMS,
        cost_estimate=cost(count, chunks),
        name="fold",
    )(*operands)


def last_kernel(n_new, n_all, away, q_ref, *refs):
    chunks = refs[:n_all]
    row_refs = refs[n_all : n_all + 3]
    acc_out, stats_out = refs[n_all + 3 :]
    half = q_ref.shape[0] // 2
    start = half if away else 0

    def finish(state, cols):
        top, total, acc = state
        acc_out[:, cols] = (acc / total).astype(jnp.bfloat16) if away else acc
        stats_out[0:1, cols] = top
        stats_out[1:2, cols] = total

    def tile(at):
        cols = pl.ds(start + at, WIDTH)
        state = tuple(r[:, cols] for r in row_refs)
        for chunk in chunks[:n_new]:
            state = fold_chunk(q_ref[cols, :], chunk, state, False)
        finish(state, pl.ds(at, WIDTH))

    each_tile(half, WIDTH, tile)

    @pl.when(jnp.logical_not(jnp.max(stats_out[1:2, :]) < LIMIT))
    def _():
        def again(at):
            q = q_ref[pl.ds(start + at, TILE), :]
            row = jnp.zeros((1, TILE), jnp.float32)
            state = (row - jnp.inf, row, jnp.zeros((DH, TILE), jnp.float32))
            for chunk in chunks:
                state = lax.fori_loop(
                    0,
                    chunk.shape[0],
                    lambda i, s, c=chunk: fold_chunk(q, c.at[pl.ds(i, 1)], s, True),
                    state,
                )
            finish(state, pl.ds(at, TILE))

        each_tile(half, TILE, again)


def last(q, new, old, state, away):
    half = q.shape[0] // 2
    operands = (q, *new, *old, *state)
    return pl.pallas_call(
        functools.partial(last_kernel, len(new), len(new) + len(old), away),
        out_shape=(
            jax.ShapeDtypeStruct((DH, half), jnp.bfloat16 if away else jnp.float32),
            jax.ShapeDtypeStruct((2, half), jnp.float32),
        ),
        in_specs=[VMEM] * len(operands),
        out_specs=[VMEM] * 2,
        compiler_params=PARAMS,
        cost_estimate=cost(half, new),
        name="last_away" if away else "last_own",
    )(*operands)


def join_kernel(own_ref, own_stats_ref, other_ref, other_stats_ref, out_ref):
    own_top, own_total = own_stats_ref[0:1, :], own_stats_ref[1:2, :]
    other_top, other_total = other_stats_ref[0:1, :], other_stats_ref[1:2, :]
    top = jnp.maximum(own_top, other_top)
    own_scale = jnp.exp2(own_top - top)
    other_scale = other_total * jnp.exp2(other_top - top)
    total = own_total * own_scale + other_scale
    joined = (
        own_ref[...] * own_scale + other_ref[...].astype(jnp.float32) * other_scale
    ) / total
    out_ref[...] = joined.T.astype(jnp.bfloat16)


def join(own, own_stats, other, other_stats):
    return pl.pallas_call(
        join_kernel,
        out_shape=jax.ShapeDtypeStruct(own.shape[::-1], jnp.bfloat16),
        in_specs=[VMEM] * 4,
        out_specs=VMEM,
        compiler_params=PARAMS,
        name="join",
    )(own, own_stats, other, other_stats)


def shift(block, axis, distance, size):
    return lax.ppermute(block, axis, [(i, (i + distance) % size) for i in range(size)])


def shards(token_queries, token_keys, token_values):
    shape = token_queries.shape
    heads = shape[0]
    flat = [a.reshape(heads, TOKENS, DH) for a in (token_queries, token_keys, token_values)]
    sent = jnp.concatenate(flat, axis=1)
    got = lax.all_to_all(sent, PLANE, split_axis=0, concat_axis=0, tiled=True)
    own_q = got[:, :TOKENS].reshape(heads * TOKENS, DH)
    chunk_a = got[: heads // 2, TOKENS:]
    chunk_b = got[heads // 2 :, TOKENS:]
    other_q = shift(own_q, "core", 1, 2)
    q = jnp.concatenate([own_q, other_q], axis=0)

    right_a, left_b = shift(chunk_a, "z", 1, RING), shift(chunk_b, "z", -1, RING)
    q, chunk_a, chunk_b = lax.optimization_barrier((q, chunk_a, chunk_b))
    right_b, left_a = shift(chunk_b, "z", 1, RING), shift(chunk_a, "z", -1, RING)
    state = fold(q, (chunk_a, chunk_b), None)
    seen = [chunk_a, chunk_b]
    for step in range(1, RING // 2):
        if step > 1:
            right_a, left_b = shift(right_a, "z", 1, RING), shift(left_b, "z", -1, RING)
            right_b, left_a = shift(right_b, "z", 1, RING), shift(left_a, "z", -1, RING)
        right_a, left_b, state = lax.optimization_barrier((right_a, left_b, state))
        state = fold(q, (right_a, left_b), state)
        right_b, left_a, state = lax.optimization_barrier((right_b, left_a, state))
        state = fold(q, (right_b, left_a), state)
        seen += [right_a, left_b, right_b, left_a]
    right_a, left_b = shift(right_a, "z", 1, RING), shift(left_b, "z", -1, RING)
    away, away_stats = last(q, (right_a, left_b), seen, state, True)
    other, other_stats = shift((away, away_stats), "core", 1, 2)
    own, own_stats = last(q, (right_a, left_b), seen, state, False)
    rows = join(own, own_stats, other, other_stats)
    back = lax.all_to_all(
        rows.reshape(shape), PLANE, split_axis=0, concat_axis=0, tiled=True
    )
    return back


def solution(mesh):
    fine = Mesh(mesh.devices.reshape(SIZES), AXES)
    placed = P(None, None, ("x", "yl", "core"), ("z", "yh"), None)
    return jax.shard_map(
        shards,
        mesh=fine,
        in_specs=(placed, placed, placed),
        out_specs=placed,
        check_vma=False,
    )
```

```python
import functools

import jax
import jax.numpy as jnp
from jax import lax
from jax.experimental import pallas as pl
from jax.experimental.pallas import tpu as pltpu
from jax.sharding import Mesh, PartitionSpec as P

AXES = ("x", "yl", "core", "z", "yh")
SIZES = (4, 2, 2, 8, 2)
PLANE = ("yh", "x", "yl")
RING = 8
DH = 128
TOKENS = 64
LOG2E = 1.4426950408889634
FACTOR = DH ** (-0.5) * LOG2E
LIMIT = 2.0**100
TILE = 128
WIDTH = 1024
COST_SCALE = 10
VMEM = pl.BlockSpec(memory_space=pltpu.VMEM)
PARAMS = pltpu.CompilerParams(vmem_limit_bytes=28 << 20)


def dot(left, right, left_dim, right_dim):
    return lax.dot_general(
        left,
        right,
        (((left_dim,), (right_dim,)), ((), ())),
        preferred_element_type=jnp.float32,
    )


def fold_chunk(q, chunk_ref, state, exact):
    keys = chunk_ref[:, :TOKENS, :].reshape(-1, DH)
    values = chunk_ref[:, TOKENS:, :].reshape(-1, DH)
    scores = dot(keys, q, 1, 1)
    shift_row = None if state is None else state[0]
    shrink = None
    if exact:
        top = jnp.max(scores, axis=0, keepdims=True) * FACTOR
        if state is not None:
            top = jnp.maximum(shift_row, top)
            shrink = jnp.exp2(shift_row - top)
        shift_row = top
    weights = jnp.exp2(scores * FACTOR - shift_row)
    total = jnp.sum(weights, axis=0, keepdims=True)
    mixed = dot(values, weights.astype(jnp.bfloat16), 0, 0)
    if state is None:
        return (shift_row, total, mixed)
    if shrink is None:
        return (shift_row, state[1] + total, state[2] + mixed)
    return (shift_row, state[1] * shrink + total, state[2] * shrink + mixed)


def cost(queries, chunks):
    keys = sum(c.shape[0] * TOKENS for c in chunks)
    return pl.CostEstimate(
        flops=COST_SCALE * queries * keys * DH,
        bytes_accessed=4 * keys * DH,
        transcendentals=0,
    )


def each_tile(count, width, body):
    def step(i, carry):
        body(pl.multiple_of(i * width, width))
        return carry

    lax.fori_loop(0, count // width, step, 0)


def fold_kernel(n_chunks, first, q_ref, *refs):
    chunks = refs[:n_chunks]

    def tile(at):
        cols = pl.ds(at, WIDTH)
        state = None if first else tuple(r[:, cols] for r in refs[n_chunks : n_chunks + 3])
        for chunk in chunks:
            state = fold_chunk(q_ref[cols, :], chunk, state, state is None)
        for ref, value in zip(refs[-3:], state):
            ref[:, cols] = value

    each_tile(q_ref.shape[0], WIDTH, tile)


def fold(q, chunks, state):
    count = q.shape[0]
    first = state is None
    operands = (q, *chunks) + (() if first else tuple(state))
    base = 1 + len(chunks)
    row = jax.ShapeDtypeStruct((1, count), jnp.float32)
    return pl.pallas_call(
        functools.partial(fold_kernel, len(chunks), first),
        out_shape=(row, row, jax.ShapeDtypeStruct((DH, count), jnp.float32)),
        in_specs=[VMEM] * len(operands),
        out_specs=[VMEM] * 3,
        input_output_aliases={} if first else {base: 0, base + 1: 1, base + 2: 2},
        compiler_params=PARAMS,
        cost_estimate=cost(count, chunks),
        name="fold",
    )(*operands)


def last_kernel(n_new, n_all, away, q_ref, *refs):
    chunks = refs[:n_all]
    row_refs = refs[n_all : n_all + 3]
    acc_out, stats_out = refs[n_all + 3 :]
    half = q_ref.shape[0] // 2
    start = half if away else 0

    def finish(state, cols):
        top, total, acc = state
        acc_out[:, cols] = (acc / total).astype(jnp.bfloat16) if away else acc
        stats_out[0:1, cols] = top
        stats_out[1:2, cols] = total

    def tile(at):
        cols = pl.ds(start + at, WIDTH)
        state = tuple(r[:, cols] for r in row_refs)
        for chunk in chunks[:n_new]:
            state = fold_chunk(q_ref[cols, :], chunk, state, False)
        finish(state, pl.ds(at, WIDTH))

    each_tile(half, WIDTH, tile)

    @pl.when(jnp.logical_not(jnp.max(stats_out[1:2, :]) < LIMIT))
    def _():
        def again(at):
            q = q_ref[pl.ds(start + at, TILE), :]
            row = jnp.zeros((1, TILE), jnp.float32)
            state = (row - jnp.inf, row, jnp.zeros((DH, TILE), jnp.float32))
            for chunk in chunks:
                state = lax.fori_loop(
                    0,
                    chunk.shape[0],
                    lambda i, s, c=chunk: fold_chunk(q, c.at[pl.ds(i, 1)], s, True),
                    state,
                )
            finish(state, pl.ds(at, TILE))

        each_tile(half, TILE, again)


def last(q, new, old, state, away):
    half = q.shape[0] // 2
    operands = (q, *new, *old, *state)
    return pl.pallas_call(
        functools.partial(last_kernel, len(new), len(new) + len(old), away),
        out_shape=(
            jax.ShapeDtypeStruct((DH, half), jnp.bfloat16 if away else jnp.float32),
            jax.ShapeDtypeStruct((2, half), jnp.float32),
        ),
        in_specs=[VMEM] * len(operands),
        out_specs=[VMEM] * 2,
        compiler_params=PARAMS,
        cost_estimate=cost(half, new),
        name="last_away" if away else "last_own",
    )(*operands)


def join_kernel(own_ref, own_stats_ref, other_ref, other_stats_ref, out_ref):
    own_top, own_total = own_stats_ref[0:1, :], own_stats_ref[1:2, :]
    other_top, other_total = other_stats_ref[0:1, :], other_stats_ref[1:2, :]
    top = jnp.maximum(own_top, other_top)
    own_scale = jnp.exp2(own_top - top)
    other_scale = other_total * jnp.exp2(other_top - top)
    total = own_total * own_scale + other_scale
    joined = (
        own_ref[...] * own_scale + other_ref[...].astype(jnp.float32) * other_scale
    ) / total
    out_ref[...] = joined.T.astype(jnp.bfloat16)


def join(own, own_stats, other, other_stats):
    return pl.pallas_call(
        join_kernel,
        out_shape=jax.ShapeDtypeStruct(own.shape[::-1], jnp.bfloat16),
        in_specs=[VMEM] * 4,
        out_specs=VMEM,
        compiler_params=PARAMS,
        name="join",
    )(own, own_stats, other, other_stats)


def shift(block, axis, distance, size):
    return lax.ppermute(block, axis, [(i, (i + distance) % size) for i in range(size)])


def shards(token_queries, token_keys, token_values):
    shape = token_queries.shape
    heads = shape[0]
    flat = [a.reshape(heads, TOKENS, DH) for a in (token_queries, token_keys, token_values)]
    sent = jnp.concatenate(flat, axis=1)
    got = lax.all_to_all(sent, PLANE, split_axis=0, concat_axis=0, tiled=True)
    own_q = got[:, :TOKENS].reshape(heads * TOKENS, DH)
    chunk_a = got[: heads // 2, TOKENS:]
    chunk_b = got[heads // 2 :, TOKENS:]
    other_q = shift(own_q, "core", 1, 2)
    q = jnp.concatenate([own_q, other_q], axis=0)

    right_a, left_b = shift(chunk_a, "z", 1, RING), shift(chunk_b, "z", -1, RING)
    q, chunk_a, chunk_b = lax.optimization_barrier((q, chunk_a, chunk_b))
    right_b, left_a = shift(chunk_b, "z", 1, RING), shift(chunk_a, "z", -1, RING)
    state = fold(q, (chunk_a, chunk_b), None)
    seen = [chunk_a, chunk_b]
    for step in range(1, RING // 2):
        if step > 1:
            right_a, left_b = shift(right_a, "z", 1, RING), shift(left_b, "z", -1, RING)
            right_b, left_a = shift(right_b, "z", 1, RING), shift(left_a, "z", -1, RING)
        right_a, left_b, state = lax.optimization_barrier((right_a, left_b, state))
        state = fold(q, (right_a, left_b), state)
        right_b, left_a, state = lax.optimization_barrier((right_b, left_a, state))
        state = fold(q, (right_b, left_a), state)
        seen += [right_a, left_b, right_b, left_a]
    right_a, left_b = shift(right_a, "z", 1, RING), shift(left_b, "z", -1, RING)
    away, away_stats = last(q, (right_a, left_b), seen, state, True)
    other, other_stats = shift((away, away_stats), "core", 1, 2)
    own, own_stats = last(q, (right_a, left_b), seen, state, False)
    rows = join(own, own_stats, other, other_stats)
    back = lax.all_to_all(
        rows.reshape(shape), PLANE, split_axis=0, concat_axis=0, tiled=True
    )
    return back


def solution(mesh):
    fine = Mesh(mesh.devices.reshape(SIZES), AXES)
    placed = P(None, None, ("x", "yl", "core"), ("z", "yh"), None)
    return jax.shard_map(
        shards,
        mesh=fine,
        in_specs=(placed, placed, placed),
        out_specs=placed,
        check_vma=False,
    )
```

```python
import functools

import jax
import jax.numpy as jnp
from jax import lax
from jax.experimental import pallas as pl
from jax.experimental.pallas import tpu as pltpu
from jax.sharding import Mesh, PartitionSpec as P

AXES = ("x", "yl", "core", "z", "yh")
SIZES = (4, 2, 2, 8, 2)
PLANE = ("yh", "x", "yl")
RING = 8
DH = 128
TOKENS = 64
LOG2E = 1.4426950408889634
FACTOR = DH ** (-0.5) * LOG2E
LIMIT = 2.0**100
TILE = 128
WIDTH = 2048
COST_SCALE = 10
VMEM = pl.BlockSpec(memory_space=pltpu.VMEM)
PARAMS = pltpu.CompilerParams(vmem_limit_bytes=28 << 20)


def dot(left, right, left_dim, right_dim):
    return lax.dot_general(
        left,
        right,
        (((left_dim,), (right_dim,)), ((), ())),
        preferred_element_type=jnp.float32,
    )


def fold_chunk(q, chunk_ref, state, exact):
    keys = chunk_ref[:, :TOKENS, :].reshape(-1, DH)
    values = chunk_ref[:, TOKENS:, :].reshape(-1, DH)
    scores = dot(keys, q, 1, 1)
    shift_row = None if state is None else state[0]
    shrink = None
    if exact:
        top = jnp.max(scores, axis=0, keepdims=True) * FACTOR
        if state is not None:
            top = jnp.maximum(shift_row, top)
            shrink = jnp.exp2(shift_row - top)
        shift_row = top
    weights = jnp.exp2(scores * FACTOR - shift_row)
    total = jnp.sum(weights, axis=0, keepdims=True)
    mixed = dot(values, weights.astype(jnp.bfloat16), 0, 0)
    if state is None:
        return (shift_row, total, mixed)
    if shrink is None:
        return (shift_row, state[1] + total, state[2] + mixed)
    return (shift_row, state[1] * shrink + total, state[2] * shrink + mixed)


def cost(queries, chunks):
    keys = sum(c.shape[0] * TOKENS for c in chunks)
    return pl.CostEstimate(
        flops=COST_SCALE * queries * keys * DH,
        bytes_accessed=4 * keys * DH,
        transcendentals=0,
    )


def each_tile(count, width, body):
    def step(i, carry):
        body(pl.multiple_of(i * width, width))
        return carry

    lax.fori_loop(0, count // width, step, 0)


def fold_kernel(n_chunks, first, q_ref, *refs):
    chunks = refs[:n_chunks]

    def tile(at):
        cols = pl.ds(at, WIDTH)
        state = None if first else tuple(r[:, cols] for r in refs[n_chunks : n_chunks + 3])
        for chunk in chunks:
            state = fold_chunk(q_ref[cols, :], chunk, state, state is None)
        for ref, value in zip(refs[-3:], state):
            ref[:, cols] = value

    each_tile(q_ref.shape[0], WIDTH, tile)


def fold(q, chunks, state):
    count = q.shape[0]
    first = state is None
    operands = (q, *chunks) + (() if first else tuple(state))
    base = 1 + len(chunks)
    row = jax.ShapeDtypeStruct((1, count), jnp.float32)
    return pl.pallas_call(
        functools.partial(fold_kernel, len(chunks), first),
        out_shape=(row, row, jax.ShapeDtypeStruct((DH, count), jnp.float32)),
        in_specs=[VMEM] * len(operands),
        out_specs=[VMEM] * 3,
        input_output_aliases={} if first else {base: 0, base + 1: 1, base + 2: 2},
        compiler_params=PARAMS,
        cost_estimate=cost(count, chunks),
        name="fold",
    )(*operands)


def last_kernel(n_new, n_all, away, q_ref, *refs):
    chunks = refs[:n_all]
    row_refs = refs[n_all : n_all + 3]
    acc_out, stats_out = refs[n_all + 3 :]
    half = q_ref.shape[0] // 2
    start = half if away else 0

    def finish(state, cols):
        top, total, acc = state
        acc_out[:, cols] = (acc / total).astype(jnp.bfloat16) if away else acc
        stats_out[0:1, cols] = top
        stats_out[1:2, cols] = total

    def tile(at):
        cols = pl.ds(start + at, min(WIDTH, half))
        state = tuple(r[:, cols] for r in row_refs)
        for chunk in chunks[:n_new]:
            state = fold_chunk(q_ref[cols, :], chunk, state, False)
        finish(state, pl.ds(at, min(WIDTH, half)))

    each_tile(half, min(WIDTH, half), tile)

    @pl.when(jnp.logical_not(jnp.max(stats_out[1:2, :]) < LIMIT))
    def _():
        def again(at):
            q = q_ref[pl.ds(start + at, TILE), :]
            row = jnp.zeros((1, TILE), jnp.float32)
            state = (row - jnp.inf, row, jnp.zeros((DH, TILE), jnp.float32))
            for chunk in chunks:
                state = lax.fori_loop(
                    0,
                    chunk.shape[0],
                    lambda i, s, c=chunk: fold_chunk(q, c.at[pl.ds(i, 1)], s, True),
                    state,
                )
            finish(state, pl.ds(at, TILE))

        each_tile(half, TILE, again)


def last(q, new, old, state, away):
    half = q.shape[0] // 2
    operands = (q, *new, *old, *state)
    return pl.pallas_call(
        functools.partial(last_kernel, len(new), len(new) + len(old), away),
        out_shape=(
            jax.ShapeDtypeStruct((DH, half), jnp.bfloat16 if away else jnp.float32),
            jax.ShapeDtypeStruct((2, half), jnp.float32),
        ),
        in_specs=[VMEM] * len(operands),
        out_specs=[VMEM] * 2,
        compiler_params=PARAMS,
        cost_estimate=cost(half, new),
        name="last_away" if away else "last_own",
    )(*operands)


def join_kernel(own_ref, own_stats_ref, other_ref, other_stats_ref, out_ref):
    own_top, own_total = own_stats_ref[0:1, :], own_stats_ref[1:2, :]
    other_top, other_total = other_stats_ref[0:1, :], other_stats_ref[1:2, :]
    top = jnp.maximum(own_top, other_top)
    own_scale = jnp.exp2(own_top - top)
    other_scale = other_total * jnp.exp2(other_top - top)
    total = own_total * own_scale + other_scale
    joined = (
        own_ref[...] * own_scale + other_ref[...].astype(jnp.float32) * other_scale
    ) / total
    out_ref[...] = joined.T.astype(jnp.bfloat16)


def join(own, own_stats, other, other_stats):
    return pl.pallas_call(
        join_kernel,
        out_shape=jax.ShapeDtypeStruct(own.shape[::-1], jnp.bfloat16),
        in_specs=[VMEM] * 4,
        out_specs=VMEM,
        compiler_params=PARAMS,
        name="join",
    )(own, own_stats, other, other_stats)


def shift(block, axis, distance, size):
    return lax.ppermute(block, axis, [(i, (i + distance) % size) for i in range(size)])


def shards(token_queries, token_keys, token_values):
    shape = token_queries.shape
    heads = shape[0]
    flat = [a.reshape(heads, TOKENS, DH) for a in (token_queries, token_keys, token_values)]
    sent = jnp.concatenate(flat, axis=1)
    got = lax.all_to_all(sent, PLANE, split_axis=0, concat_axis=0, tiled=True)
    own_q = got[:, :TOKENS].reshape(heads * TOKENS, DH)
    chunk_a = got[: heads // 2, TOKENS:]
    chunk_b = got[heads // 2 :, TOKENS:]
    other_q = shift(own_q, "core", 1, 2)
    q = jnp.concatenate([own_q, other_q], axis=0)

    right_a, left_b = shift(chunk_a, "z", 1, RING), shift(chunk_b, "z", -1, RING)
    q, chunk_a, chunk_b = lax.optimization_barrier((q, chunk_a, chunk_b))
    right_b, left_a = shift(chunk_b, "z", 1, RING), shift(chunk_a, "z", -1, RING)
    state = fold(q, (chunk_a, chunk_b), None)
    seen = [chunk_a, chunk_b]
    for step in range(1, RING // 2):
        if step > 1:
            right_a, left_b = shift(right_a, "z", 1, RING), shift(left_b, "z", -1, RING)
            right_b, left_a = shift(right_b, "z", 1, RING), shift(left_a, "z", -1, RING)
        right_a, left_b, state = lax.optimization_barrier((right_a, left_b, state))
        state = fold(q, (right_a, left_b), state)
        right_b, left_a, state = lax.optimization_barrier((right_b, left_a, state))
        state = fold(q, (right_b, left_a), state)
        seen += [right_a, left_b, right_b, left_a]
    right_a, left_b = shift(right_a, "z", 1, RING), shift(left_b, "z", -1, RING)
    away, away_stats = last(q, (right_a, left_b), seen, state, True)
    other, other_stats = shift((away, away_stats), "core", 1, 2)
    own, own_stats = last(q, (right_a, left_b), seen, state, False)
    rows = join(own, own_stats, other, other_stats)
    back = lax.all_to_all(
        rows.reshape(shape), PLANE, split_axis=0, concat_axis=0, tiled=True
    )
    return back


def solution(mesh):
    fine = Mesh(mesh.devices.reshape(SIZES), AXES)
    placed = P(None, None, ("x", "yl", "core"), ("z", "yh"), None)
    return jax.shard_map(
        shards,
        mesh=fine,
        in_specs=(placed, placed, placed),
        out_specs=placed,
        check_vma=False,
    )
```
